256 devices in a mesh: shot: 16 (over y, x_hi, core), slab: 16 (over z, x_lo).
Axes of the slice: x: 4 (x_hi: 2, x_lo: 2; x = x_hi * 2 + x_lo), y: 4, z: 8, core: 2. Of those that a mesh axis runs over, the one named last changes fastest.
Arguments:
- state_before: float32 [16, 256, 128, 128], P('shot', 'slab'), may hold values from -6 to 6
- state_now: float32 [16, 256, 128, 128], P('shot', 'slab'), may hold values from -6 to 6
- adjoint_after: float32 [16, 256, 128, 128], P('shot', 'slab'), may hold values from -6 to 6
- adjoint_now: float32 [16, 256, 128, 128], P('shot', 'slab'), may hold values from -6 to 6
- speed_term: float32 [256, 128, 128], P('slab'), may hold values from 0.04 to 0.18
- wavelet: float32 [16, 8], P('shot'), may hold values from -180 to 180
- source: int32 [16, 3], P('shot'), may hold values from 0 to 255, as said below
- receivers: int32 [16, 3, 4096], P('shot'), may hold values from 0 to 255, as said below
- traces: float32 [16, 8, 4096], P('shot', None, 'slab'), may hold values from -6 to 6
Outputs:
- adj_first: float32 [16, 256, 128, 128], P('shot', 'slab')
- adj_second: float32 [16, 256, 128, 128], P('shot', 'slab')
- gradient: float32 [256, 128, 128], P('slab', 'shot')
The draws below stay inside these ranges and needn't reach their ends.
Inputs may be any that keep to these rules, and one draw needn't show every extreme that they name: `source`: row 0 is a depth row below 256, row 1 a cell below 128, row 2 a cell below 128. `receivers`: row 0 is a depth row below 256, row 1 a cell below 128, row 2 a cell below 128; several receivers may share a cell.
All inputs are finite; a program needn't handle non-finite values.
Results may differ from the reference program's by a relative error of at most 0.0003.
Values sent between devices are 32-bit elements; how exact they have to be, the bound alone decides.
A program may use at most 128 MiB of HBM per device.

```python
import math
import jax
import jax.numpy as jnp
from jax import lax

NY = 128
NZ = 128
STEPS = 8
NX = 256
RECV = 4096
SHOTS = 16


def draw_source(key, part):
    keys = jax.random.split(key, 3)
    depth = jax.random.randint(keys[0], (SHOTS,), 0, NX)
    across = jax.random.randint(keys[1], (SHOTS,), 0, NY)
    along = jax.random.randint(keys[2], (SHOTS,), 0, NZ)
    return jnp.stack((depth, across, along), axis=1).astype(jnp.int32)


def draw_receivers(key, part):
    keys = jax.random.split(key, 4)
    depth = jnp.minimum(jax.random.randint(keys[0], (SHOTS, RECV), 0, NX), jax.random.randint(keys[1], (SHOTS, RECV), 0, NX))
    across = jax.random.randint(keys[2], (SHOTS, RECV), 0, NY)
    along = jax.random.randint(keys[3], (SHOTS, RECV), 0, NZ)
    return jnp.stack((depth, across, along), axis=1).astype(jnp.int32)


def level_of(stream_key, extent, cuts, least, largest):
    factor_of, own = 1.0, jax.random.fold_in(stream_key, 6)
    for dim, parts in cuts:
        draws = jnp.exp(jax.random.uniform(jax.random.fold_in(own, dim), (parts,), jnp.float32, least / len(cuts), largest / len(cuts)))
        factor_of = factor_of * jnp.repeat(draws, extent[dim] // parts).reshape([-1 if axis == dim else 1 for axis in range(len(extent))])
    return factor_of


def scatter_about(key, shape, spread, reach, shards=(), held_as=jnp.bfloat16):
    array = jax.random.normal(key, shape, jnp.float32) * spread
    if len(shards) > 0:
        array = level_of(key, shape, shards, -0.22, 0.18) * array
    return jnp.clip(array, min=-reach, max=reach).astype(held_as)


def setup_inputs(seed: int = 0) -> dict:
    splits = jax.random.split(jax.random.key(seed), 10)
    return {
        "state_before": scatter_about(splits[0], (SHOTS, NX, NY, NZ), 1.0, 6.0, ((0, 16), (1, 16)), jnp.float32),
        "state_now": scatter_about(splits[1], (SHOTS, NX, NY, NZ), 1.0, 6.0, ((0, 16), (1, 16)), jnp.float32),
        "adjoint_after": scatter_about(splits[2], (SHOTS, NX, NY, NZ), 1.0, 6.0, ((0, 16), (1, 16)), jnp.float32),
        "adjoint_now": scatter_about(splits[3], (SHOTS, NX, NY, NZ), 1.0, 6.0, ((0, 16), (1, 16)), jnp.float32),
        "speed_term": jnp.clip(jnp.exp(math.log(0.18) - 1.50407746 * jax.random.uniform(splits[4], (NX, NY, NZ), jnp.float32) ** level_of(splits[4], (NX, NY, NZ), ((0, 16),), -0.2, 0.2)), 0.04, 0.18),
        "wavelet": scatter_about(splits[5], (SHOTS, STEPS), 30.0, 180.0, ((0, 16),), jnp.float32),
        "source": draw_source(jax.random.fold_in(splits[9], 71), 0),
        "receivers": draw_receivers(jax.random.fold_in(splits[9], 71), 0),
        "traces": scatter_about(splits[8], (SHOTS, STEPS, RECV), 1.0, 6.0, ((0, 16), (2, 16)), jnp.float32),
    }


stencil_weights = (-205.0 / 72.0, 8.0 / 5.0, -1.0 / 5.0, 8.0 / 315.0, -1.0 / 560.0)


def laplace(extended):
    count = extended.shape[0] - 8
    width_y = extended.shape[1]
    width_z = extended.shape[2]
    centre = extended[4:4 + count]
    sided = jnp.pad(centre, ((0, 0), (4, 4), (4, 4)))
    total = (3.0 * stencil_weights[0]) * centre
    for step in range(1, 5):
        near = extended[4 + step:4 + step + count] + extended[4 - step:4 - step + count]
        near = near + sided[:, 4 + step:4 + step + width_y, 4:4 + width_z] + sided[:, 4 - step:4 - step + width_y, 4:4 + width_z]
        near = near + sided[:, 4:4 + width_y, 4 + step:4 + step + width_z] + sided[:, 4:4 + width_y, 4 - step:4 - step + width_z]
        total = total + stencil_weights[step] * near
    return total


def lap_zero(field):
    return laplace(jnp.pad(field, ((4, 4), (0, 0), (0, 0))))


def add_cells(field, flat, values):
    shape = field.shape
    return field.reshape(-1).at[flat].add(values).reshape(shape)


def reference(state_before, state_now, adjoint_after, adjoint_now, speed_term, wavelet, source, receivers, traces):
    scale = 1.0 / (8.0 * STEPS)

    def one_shot(grad, inputs):
        before, now, after, adj_now, wave, spot, recv, trace = inputs
        spot_flat = (spot[0] * (NY * NZ) + spot[1] * NZ + spot[2]).astype(jnp.int32)
        recv_flat = (recv[0] * (NY * NZ) + recv[1] * NZ + recv[2]).astype(jnp.int32)

        def forward(carry, amount):
            prev, cur = carry
            lapl = lap_zero(cur)
            nxt = add_cells(2.0 * cur - prev + speed_term * lapl, spot_flat, amount)
            return (cur, nxt), lapl

        _, stored = lax.scan(forward, (before, now), wave)

        def backward(carry, inputs):
            later, cur, total = carry
            lapl_t, row = inputs
            nxt = add_cells(2.0 * cur - later + speed_term * lap_zero(cur), recv_flat, row)
            return (cur, nxt, total + cur * lapl_t), None

        zero = jnp.zeros(now.shape, jnp.float32)
        (second, first, total), _ = lax.scan(backward, (after, adj_now, zero), (stored, trace), reverse=True)
        return grad + total * scale, (first, second)

    grad0 = jnp.zeros((NX, NY, NZ), jnp.float32)
    gradient, (firsts, seconds) = lax.scan(one_shot, grad0, (state_before, state_now, adjoint_after, adjoint_now, wavelet, source, receivers, traces))
    return firsts, seconds, gradient
```

```python
import functools

import numpy as np
import jax
import jax.numpy as jnp
from jax import lax
from jax.experimental import pallas as pl
from jax.experimental.pallas import tpu as pltpu
from jax.sharding import PartitionSpec as P

MESH = pl.DeviceIdType.MESH
F32 = jnp.float32
BF16 = jnp.bfloat16

UNIT = 8.0 / 5.0
CENTRE = 3.0 * (-205.0 / 72.0) / UNIT
FAR = 1.0 / 63.0
EDGE = 4


def band(width):
    gap = np.abs(np.arange(width)[:, None] - np.arange(width)[None, :])
    near = np.where(gap == 1, 1.0, 0.0) + np.where(gap == 2, -1.0 / 8.0, 0.0)
    far = np.where(gap == 3, 1.0, 0.0) + np.where(gap == 4, -9.0 / 128.0, 0.0)
    row = np.concatenate([near, far], axis=1)
    return np.concatenate([row, row], axis=0)


def place():
    shot = lax.axis_index("shot")
    slab = lax.axis_index("slab")
    return shot, slab, lax.rem(shot, 2), lax.rem(slab, 2)


def gather_kernel(slabs, traces, cells, all_traces, all_cells, send, recv, own, pack_send, pack_recv, pack_own):
    shot, slab, core, side = place()
    half = slabs // 2
    z = lax.div(slab, 2)
    stays = core == side
    barrier = pltpu.get_barrier_semaphore()

    @pl.loop(0, slabs)
    def _(k):
        @pl.when(jnp.logical_or(core != side, k != slab))
        def _():
            pl.semaphore_signal(barrier, inc=1, device_id=(shot - core + side, k), device_id_type=MESH)

    pl.semaphore_wait(barrier, jnp.where(stays, slabs - 1, slabs))

    def outgoing(k):
        to_core, to_z = lax.div(k, half), lax.rem(k, half)
        return pltpu.make_async_remote_copy(
            src_ref=traces,
            dst_ref=all_traces.at[slab],
            send_sem=send.at[k],
            recv_sem=recv.at[slab],
            device_id=(shot - core + to_core, 2 * to_z + core),
            device_id_type=MESH,
        )

    def is_me(k):
        return jnp.logical_and(stays, k == core * half + z)

    mine = pltpu.make_async_copy(traces, all_traces.at[slab], own.at[0])
    pack = pltpu.make_async_remote_copy(
        src_ref=cells,
        dst_ref=all_cells,
        send_sem=pack_send.at[0],
        recv_sem=pack_recv.at[0],
        device_id=(shot + 1 - 2 * core, slab),
        device_id_type=MESH,
    )
    pack_mine = pltpu.make_async_copy(cells, all_cells, pack_own.at[0])

    @pl.when(stays)
    def _():
        pack.start()
        pack_mine.start()
        mine.start()

    @pl.loop(0, slabs)
    def _(k):
        @pl.when(jnp.logical_not(is_me(k)))
        def _():
            outgoing(k).start()

    @pl.loop(0, slabs)
    def _(k):
        @pl.when(jnp.logical_or(core != side, k != slab))
        def _():
            pltpu.make_async_remote_copy(
                src_ref=traces,
                dst_ref=all_traces.at[k],
                send_sem=send.at[k],
                recv_sem=recv.at[k],
                device_id=(shot - core + side, k),
                device_id_type=MESH,
            ).wait_recv()

    @pl.loop(0, slabs)
    def _(k):
        @pl.when(jnp.logical_not(is_me(k)))
        def _():
            outgoing(k).wait_send()

    @pl.when(stays)
    def _():
        pack.wait_send()
        pack_mine.wait()
        mine.wait()

    @pl.when(jnp.logical_not(stays))
    def _():
        pack.wait_recv()


def inject_kernel(cells, keys, traces, out, listed):
    @pl.loop(0, cells // 16)
    def _(i):
        out[pl.ds(pl.multiple_of(i * 128, 128), 128), :] = jnp.zeros((128, 128), F32)

    rows, lanes = keys.shape

    def compact(i, count):
        for u in range(16):
            key = keys[lax.shift_right_logical(i, 3), jnp.bitwise_and(i, 7) * 16 + u]
            listed[count] = key
            count = count + jnp.where(key >= 0, 1, 0).astype(jnp.int32)
        return count

    count = lax.fori_loop(0, rows * lanes // 16, compact, jnp.int32(0))
    lane = lax.broadcasted_iota(jnp.int32, (8, 128), 1)

    def add(k, carry):
        key = listed[k]
        r = lax.shift_right_logical(key, 18)
        cell = jnp.bitwise_and(key, (1 << 18) - 1)
        z = jnp.bitwise_and(cell, 127)
        row = pl.multiple_of(lax.shift_right_logical(cell, 7) * 8, 8)
        column = pl.multiple_of(jnp.bitwise_and(lax.shift_right_logical(r, 7), 1) * 128, 128)
        values = traces[lax.shift_right_logical(r, 8), :, pl.ds(column, 128)]
        turned = pltpu.roll(values, jnp.bitwise_and(z - jnp.bitwise_and(r, 127), 127), 1)
        out[pl.ds(row, 8), :] = out[pl.ds(row, 8), :] + jnp.where(lane == z, turned, 0.0)
        return carry

    lax.fori_loop(0, count, add, jnp.int32(0))


def wave_kernel(
    shots,
    slabs,
    steps,
    scale,
    adj_now,
    adj_now_far,
    adj_after,
    adj_after_far,
    state_now,
    state_before,
    speed,
    speed_far,
    added,
    amounts,
    mark,
    weights_z,
    weights_y,
    opening,
    second,
    gradient,
    qa,
    pf,
    laps,
    inj,
    spd,
    total,
    parts,
    loads,
    swap_send,
    swap_recv,
    halo_send,
    halo_recv,
    out_send,
    out_recv,
    part_send,
    part_recv,
    part_own,
):
    shot, slab, core, side = place()
    z = lax.div(slab, 2)
    stays = core == side
    moves = core != side
    count, wide, lanes = spd.shape
    mid = count - 2 * EDGE
    last = slabs // 2 - 1
    has_outer = jnp.logical_or(jnp.logical_and(core == 0, z > 0), jnp.logical_and(core == 1, z < last))
    inner = (shot + 1 - 2 * core, slab)
    outer = (shot + 1 - 2 * core, slab + 4 * core - 2)
    partner = (shot - core + side, slab - side + core)
    chunk = wide // shots
    me = shot - core + side
    own_rows = pl.ds(EDGE, count)

    def source_of(s):
        return (s - lax.rem(s, 2) + side, 2 * z + lax.rem(s, 2))

    barrier = pltpu.get_barrier_semaphore()
    pl.semaphore_signal(barrier, inc=1, device_id=inner, device_id_type=MESH)

    @pl.when(has_outer)
    def _():
        pl.semaphore_signal(barrier, inc=1, device_id=outer, device_id_type=MESH)

    @pl.when(moves)
    def _():
        pl.semaphore_signal(barrier, inc=1, device_id=partner, device_id_type=MESH)

    @pl.loop(0, shots)
    def _(s):
        @pl.when(jnp.logical_or(moves, s != shot))
        def _():
            pl.semaphore_signal(barrier, inc=1, device_id=source_of(s), device_id_type=MESH)

    def load(k, near, far, to):
        def go():
            @pl.when(stays)
            def _():
                pltpu.make_async_copy(near, to, loads.at[k]).start()

            @pl.when(moves)
            def _():
                pltpu.make_async_copy(far, to, loads.at[k]).start()

        def done():
            pltpu.make_async_copy(near, to, loads.at[k]).wait()

        return go, done

    now_go, now_done = load(0, adj_now, adj_now_far, qa.at[1, own_rows])
    after_go, after_done = load(1, adj_after, adj_after_far, qa.at[0, own_rows])
    speed_go, speed_done = load(2, speed, speed_far, spd)
    now_go()
    speed_go()
    after_go()
    inj_copy = pltpu.make_async_copy(added, inj, loads.at[3])
    inj_copy.start()

    def swap(k, here, to):
        remote = pltpu.make_async_remote_copy(
            src_ref=here,
            dst_ref=to,
            send_sem=swap_send.at[k],
            recv_sem=swap_recv.at[k],
            device_id=partner,
            device_id_type=MESH,
        )
        local = pltpu.make_async_copy(here, to, loads.at[4 + k])

        def go():
            @pl.when(moves)
            def _():
                remote.start()

            @pl.when(stays)
            def _():
                local.start()

        def done():
            @pl.when(moves)
            def _():
                remote.wait_recv()

            @pl.when(stays)
            def _():
                local.wait()

        def sent():
            @pl.when(moves)
            def _():
                remote.wait_send()

        return go, done, sent

    p_now = swap(0, state_now, pf.at[1, own_rows])
    p_before = swap(1, state_before, pf.at[0, own_rows])

    @pl.when(jnp.logical_not(has_outer))
    def _():
        @pl.loop(0, steps)
        def _(k):
            @pl.loop(0, EDGE)
            def _(r):
                row = core * (count + EDGE) + r
                qa[k + 1, row] = jnp.zeros((wide, lanes), F32)
                pf[k + 1, row] = jnp.zeros((wide, lanes), F32)

    pl.semaphore_wait(
        barrier,
        1 + jnp.where(has_outer, 1, 0) + jnp.where(moves, 1, 0) + jnp.where(stays, shots - 1, shots),
    )

    fields = (qa, pf)

    def inner_copy(chain, slot):
        return pltpu.make_async_remote_copy(
            src_ref=fields[chain].at[slot, pl.ds(count - core * mid - core * EDGE, EDGE)],
            dst_ref=fields[chain].at[slot, pl.ds(core * (count + EDGE), EDGE)],
            send_sem=halo_send.at[chain, 0, slot],
            recv_sem=halo_recv.at[chain, 0, slot],
            device_id=inner,
            device_id_type=MESH,
        )

    def outer_copy(chain, slot):
        return pltpu.make_async_remote_copy(
            src_ref=fields[chain].at[slot, pl.ds(EDGE + core * (mid + EDGE), EDGE)],
            dst_ref=fields[chain].at[slot, pl.ds((1 - core) * (count + EDGE), EDGE)],
            send_sem=halo_send.at[chain, 1, slot],
            recv_sem=halo_recv.at[chain, 1, slot],
            device_id=outer,
            device_id_type=MESH,
        )

    def send_inner(chain, slot):
        inner_copy(chain, slot).start()

    def send_outer(chain, slot):
        @pl.when(has_outer)
        def _():
            outer_copy(chain, slot).start()

    def wait_inner(chain, slot):
        inner_copy(chain, slot).wait_recv()

    def wait_outer(chain, slot):
        @pl.when(has_outer)
        def _():
            outer_copy(chain, slot).wait_recv()

    inner_base = (1 - core) * (mid + EDGE)
    outer_base = core * (mid + EDGE)

    def lateral(field, slot, group, finish):
        x = field[slot, pl.ds(EDGE + 4 * group, 4)]
        high = x.astype(BF16)
        low = (x - high.astype(F32)).astype(BF16)
        along = jnp.concatenate([high.reshape(4 * wide, lanes), low.reshape(4 * wide, lanes)], axis=1)
        across = jnp.concatenate(
            [
                jnp.concatenate([high[i] for i in range(4)], axis=1),
                jnp.concatenate([low[i] for i in range(4)], axis=1),
            ],
            axis=0,
        )
        sums_z = jnp.dot(along, weights_z[...], preferred_element_type=F32)
        sums_y = jnp.dot(weights_y[...], across, preferred_element_type=F32)
        for i in range(4):
            near = sums_z[wide * i : wide * (i + 1), :lanes] + sums_y[:wide, lanes * i : lanes * (i + 1)]
            far = sums_z[wide * i : wide * (i + 1), lanes:] + sums_y[wide:, lanes * i : lanes * (i + 1)]
            finish(4 * group + i, x[i], near + far * FAR + CENTRE * x[i])

    def depth(field, slot, base, planes, finish):
        @pl.loop(0, wide // 8)
        def _(k):
            part = pl.ds(pl.multiple_of(8 * k, 8), 8)
            e = [field[slot, base + r, part, :] for r in range(planes + 2 * EDGE)]
            for r in range(planes):
                value = (e[r + 3] + e[r + 5]) - 0.125 * (e[r + 2] + e[r + 6])
                value = value + FAR * ((e[r + 1] + e[r + 7]) - (9.0 / 128.0) * (e[r] + e[r + 8]))
                finish(base + r, part, value)

    def lateral_a(j):
        def finish(row, x, value):
            extra = inj[pl.ds(row * (8 * wide) + (steps - 1 - j), wide, stride=8), :]
            qa[j + 2, EDGE + row] = (2.0 * x - qa[j, EDGE + row]) + extra + spd[row] * value

        @pl.loop(0, count // 4)
        def _(group):
            lateral(qa, j + 1, group, finish)

        depth_a(j, EDGE, mid)

    def depth_a(j, base, planes):
        def finish(row, part, value):
            qa[j + 2, EDGE + row, part, :] = qa[j + 2, EDGE + row, part, :] + spd[row, part, :] * value

        depth(qa, j + 1, base, planes, finish)

    def edges_a(j, more):
        wait_inner(0, j + 1)
        depth_a(j, inner_base, EDGE)
        if more is None:
            send_inner(0, j + 2)
        else:
            pl.when(more)(lambda: send_inner(0, j + 2))
        wait_outer(0, j + 1)
        depth_a(j, outer_base, EDGE)
        if more is None:
            send_outer(0, j + 2)
        else:
            pl.when(more)(lambda: send_outer(0, j + 2))

    lead = steps // 2

    def lateral_f(i, kept):
        keep = i if kept else lead

        def finish(row, x, value):
            pf[i + 2, EDGE + row] = (2.0 * x - pf[i, EDGE + row]) + amounts[i, row] * mark[...]
            laps[keep, row] = value

        @pl.loop(0, count // 4)
        def _(group):
            lateral(pf, i + 1, group, finish)

        depth_f(i, EDGE, mid, kept)

    def depth_f(i, base, planes, kept):
        keep = i if kept else lead

        def finish(row, part, value):
            lap = laps[keep, row, part, :] + value
            pf[i + 2, EDGE + row, part, :] = pf[i + 2, EDGE + row, part, :] + spd[row, part, :] * lap
            if kept:
                laps[keep, row, part, :] = lap
            else:
                total[row, part, :] = total[row, part, :] + qa[steps - i, EDGE + row, part, :] * lap

        depth(pf, i + 1, base, planes, finish)

    def edges_f(i, kept, more):
        wait_inner(1, i + 1)
        depth_f(i, inner_base, EDGE, kept)
        if more:
            send_inner(1, i + 2)
        wait_outer(1, i + 1)
        depth_f(i, outer_base, EDGE, kept)
        if more:
            send_outer(1, i + 2)

    p_now[0]()
    now_done()
    send_outer(0, 1)
    send_inner(0, 1)
    p_before[0]()
    after_done()
    speed_done()

    @pl.loop(0, count)
    def _(row):
        spd[row] = UNIT * spd[row]

    inj_copy.wait()
    lateral_a(0)

    @pl.loop(0, lead)
    def _(j):
        edges_a(j, None)
        lateral_a(j + 1)

    p_now[1]()
    send_outer(1, 1)
    send_inner(1, 1)
    p_before[1]()
    lateral_f(0, True)

    def result(k, here, to):
        remote = pltpu.make_async_remote_copy(
            src_ref=here,
            dst_ref=to,
            send_sem=out_send.at[k],
            recv_sem=out_recv.at[k],
            device_id=partner,
            device_id_type=MESH,
        )
        local = pltpu.make_async_copy(here, to, loads.at[6 + k])

        def go():
            @pl.when(moves)
            def _():
                remote.start()

            @pl.when(stays)
            def _():
                local.start()

        def done():
            @pl.when(moves)
            def _():
                remote.wait()

            @pl.when(stays)
            def _():
                local.wait()

        return go, done

    second_out = result(0, qa.at[steps, own_rows], second.at[0])
    opening_out = result(1, qa.at[steps + 1, own_rows], opening.at[0])

    @pl.loop(0, steps - lead)
    def _(m):
        j = lead + m
        edges_a(j, j < steps - 1)

        @pl.when(j == steps - 2)
        def _():
            second_out[0]()

        edges_f(m, True, True)

        @pl.when(j < steps - 1)
        def _():
            lateral_a(j + 1)

        @pl.when(m < lead - 1)
        def _():
            lateral_f(m + 1, True)

    opening_out[0]()

    @pl.loop(0, count)
    def _(row):
        sums = qa[steps, EDGE + row] * laps[0, row]
        for i in range(1, lead):
            sums = sums + qa[steps - i, EDGE + row] * laps[i, row]
        total[row] = sums

    lateral_f(lead, False)

    @pl.loop(lead, steps - 1)
    def _(i):
        edges_f(i, False, True)
        lateral_f(i + 1, False)

    spans = ((EDGE, mid), (0, EDGE), (EDGE + mid, EDGE))

    def is_me(s):
        return jnp.logical_and(stays, s == shot)

    def part_copy(n, s):
        rows = pl.ds(*spans[n])
        return pltpu.make_async_remote_copy(
            src_ref=total.at[rows, pl.ds(pl.multiple_of(chunk * s, chunk), chunk)],
            dst_ref=parts.at[me, rows],
            send_sem=part_send.at[n, s],
            recv_sem=part_recv.at[n, me],
            device_id=(s, 2 * z + core),
            device_id_type=MESH,
        )

    def part_mine(n):
        rows = pl.ds(*spans[n])
        return pltpu.make_async_copy(
            total.at[rows, pl.ds(pl.multiple_of(chunk * shot, chunk), chunk)], parts.at[me, rows], part_own.at[n]
        )

    def send_parts(n):
        @pl.when(stays)
        def _():
            part_mine(n).start()

        @pl.loop(0, shots)
        def _(k):
            s = lax.rem(shot + k, shots)

            @pl.when(jnp.logical_not(is_me(s)))
            def _():
                part_copy(n, s).start()

    def wait_parts(n):
        rows = pl.ds(*spans[n])

        @pl.when(stays)
        def _():
            part_mine(n).wait()

        @pl.loop(0, shots)
        def _(s):
            @pl.when(jnp.logical_or(moves, s != me))
            def _():
                pltpu.make_async_remote_copy(
                    src_ref=total.at[rows, pl.ds(0, chunk)],
                    dst_ref=parts.at[s, rows],
                    send_sem=part_send.at[n, s],
                    recv_sem=part_recv.at[n, s],
                    device_id=source_of(s),
                    device_id_type=MESH,
                ).wait_recv()

            @pl.when(jnp.logical_not(is_me(s)))
            def _():
                part_copy(n, s).wait_send()

    send_parts(0)
    edges_f(steps - 1, False, False)
    send_parts(1)
    send_parts(2)

    p_now[2]()
    p_before[2]()

    @pl.loop(1, steps + 1)
    def _(slot):
        for chain in range(2):
            inner_copy(chain, slot).wait_send()

            @pl.when(has_outer)
            def _():
                outer_copy(chain, slot).wait_send()

    second_out[1]()
    opening_out[1]()
    for n in range(3):
        wait_parts(n)

    @pl.loop(0, count)
    def _(row):
        sums = parts[0, row]
        for s in range(1, shots):
            sums = sums + parts[s, row]
        gradient[row] = sums * scale


def body(
    shots,
    slabs,
    state_before,
    state_now,
    adjoint_after,
    adjoint_now,
    speed_term,
    wavelet,
    source,
    receivers,
    traces,
):
    count, wide, lanes = speed_term.shape
    steps = wavelet.shape[1]
    held = traces.shape[2]
    plane = wide * lanes
    shot, slab, core, side = place()
    slab_here = slab - side + core

    over = ("shot", "slab")
    pairs, speed_pairs = [], []
    for s in range(shots):
        for k in range(slabs):
            c, d = s % 2, k % 2
            if c != d:
                pairs.append((s * slabs + k, (s - c + d) * slabs + k - d + c))
                high = (s // 2) % 2
                other = s - 2 * high + 2 * (1 - high) - c + d
                speed_pairs.append((s * slabs + k, other * slabs + k - d + c))
    now_far = lax.ppermute(adjoint_now[0], over, pairs)
    speed_far = lax.ppermute(speed_term, over, speed_pairs)
    after_far = lax.ppermute(adjoint_after[0], over, pairs)

    flat = (receivers[0, 0] * plane + receivers[0, 1] * lanes + receivers[0, 2]).reshape(-1, 128)
    spot = source[0, 0] * plane + source[0, 1] * lanes + source[0, 2]
    cells = jnp.concatenate([flat, jnp.broadcast_to(spot, (8, 128))], axis=0)
    wave = jnp.broadcast_to(wavelet[0][:, None], (steps, 128))
    packed = jnp.concatenate([traces[0], wave], axis=1)
    anywhere = pl.BlockSpec(memory_space=pl.ANY)
    in_vmem = pl.BlockSpec(memory_space=pltpu.VMEM)
    in_smem = pl.BlockSpec(memory_space=pltpu.SMEM)

    all_traces, all_cells = pl.pallas_call(
        functools.partial(gather_kernel, slabs),
        name="gather_traces",
        out_shape=(
            jax.ShapeDtypeStruct((slabs, steps, held + 128), F32),
            jax.ShapeDtypeStruct(cells.shape, jnp.int32),
        ),
        in_specs=[anywhere, anywhere],
        out_specs=(anywhere, anywhere),
        scratch_shapes=[
            pltpu.SemaphoreType.DMA((slabs,)),
            pltpu.SemaphoreType.DMA((slabs,)),
            pltpu.SemaphoreType.DMA((1,)),
            pltpu.SemaphoreType.DMA((1,)),
            pltpu.SemaphoreType.DMA((1,)),
            pltpu.SemaphoreType.DMA((1,)),
        ],
        compiler_params=pltpu.CompilerParams(collective_id=0, has_side_effects=True),
        cost_estimate=pl.CostEstimate(flops=0, bytes_accessed=20 << 20, transcendentals=0),
    )(packed, cells)

    base = slab_here * (count * plane)
    here = all_cells[:-8] - base
    order = lax.broadcasted_iota(jnp.int32, here.shape, 0) * 128 + lax.broadcasted_iota(jnp.int32, here.shape, 1)
    keys = jnp.where((here >= 0) & (here < count * plane), order * (count * plane) + here, -1)
    added = pl.pallas_call(
        functools.partial(inject_kernel, count * wide),
        name="inject",
        out_shape=jax.ShapeDtypeStruct((count * wide * steps, lanes), F32),
        in_specs=[in_smem, in_vmem],
        out_specs=in_vmem,
        scratch_shapes=[pltpu.SMEM((here.size,), jnp.int32)],
        compiler_params=pltpu.CompilerParams(vmem_limit_bytes=32 << 20),
        cost_estimate=pl.CostEstimate(flops=0, bytes_accessed=30 << 20, transcendentals=0),
    )(keys, all_traces)

    spot_here = all_cells[-1, 0] - base
    spot_row = jnp.where(spot_here < 0, -1, spot_here // plane)
    spot_cell = jnp.bitwise_and(spot_here, plane - 1)
    amounts = jnp.where(lax.broadcasted_iota(jnp.int32, (steps, count), 1) == spot_row, all_traces[0, :, held : held + 1], 0.0)
    mark_at = lax.broadcasted_iota(jnp.int32, (wide, lanes), 0) * lanes + lax.broadcasted_iota(jnp.int32, (wide, lanes), 1)
    mark = jnp.where(mark_at == spot_cell, 1.0, 0.0).astype(F32)
    weights = band(wide)

    long = count + 2 * EDGE
    opening, second, gradient = pl.pallas_call(
        functools.partial(wave_kernel, shots, slabs, steps, UNIT / (8.0 * steps)),
        name="waves",
        out_shape=(
            jax.ShapeDtypeStruct((1, count, wide, lanes), F32),
            jax.ShapeDtypeStruct((1, count, wide, lanes), F32),
            jax.ShapeDtypeStruct((count, wide // shots, lanes), F32),
        ),
        in_specs=[anywhere] * 9 + [in_smem, in_vmem, in_vmem, in_vmem],
        out_specs=(anywhere, anywhere, in_vmem),
        scratch_shapes=[
            pltpu.VMEM((steps + 2, long, wide, lanes), F32),
            pltpu.VMEM((steps + 2, long, wide, lanes), F32),
            pltpu.VMEM((steps // 2 + 1, count, wide, lanes), F32),
            pltpu.VMEM((count * wide * steps, lanes), F32),
            pltpu.VMEM((count, wide, lanes), F32),
            pltpu.VMEM((count, wide, lanes), F32),
            pltpu.VMEM((shots, count, wide // shots, lanes), F32),
            pltpu.SemaphoreType.DMA((8,)),
            pltpu.SemaphoreType.DMA((2,)),
            pltpu.SemaphoreType.DMA((2,)),
            pltpu.SemaphoreType.DMA((2, 2, steps + 2)),
            pltpu.SemaphoreType.DMA((2, 2, steps + 2)),
            pltpu.SemaphoreType.DMA((2,)),
            pltpu.SemaphoreType.DMA((2,)),
            pltpu.SemaphoreType.DMA((3, shots)),
            pltpu.SemaphoreType.DMA((3, shots)),
            pltpu.SemaphoreType.DMA((3,)),
        ],
        compiler_params=pltpu.CompilerParams(
            collective_id=1, has_side_effects=True, vmem_limit_bytes=62 << 20
        ),
    )(
        adjoint_now[0],
        now_far,
        adjoint_after[0],
        after_far,
        state_now[0],
        state_before[0],
        speed_term,
        speed_far,
        added,
        amounts,
        mark,
        jnp.asarray(weights, BF16),
        jnp.asarray(weights.T, BF16),
    )
    return opening, second, gradient


def solution(mesh):
    return jax.shard_map(
        functools.partial(body, mesh.shape["shot"], mesh.shape["slab"]),
        mesh=mesh,
        in_specs=(
            P("shot", "slab", None, None),
            P("shot", "slab", None, None),
            P("shot", "slab", None, None),
            P("shot", "slab", None, None),
            P("slab", None, None),
            P("shot", None),
            P("shot", None),
            P("shot", None, None),
            P("shot", None, "slab"),
        ),
        out_specs=(
            P("shot", "slab", None, None),
            P("shot", "slab", None, None),
            P("slab", "shot", None),
        ),
        check_vma=False,
    )
```

```python
import functools

import numpy as np
import jax
import jax.numpy as jnp
from jax import lax
from jax.experimental import pallas as pl
from jax.experimental.pallas import tpu as pltpu
from jax.sharding import PartitionSpec as P

MESH = pl.DeviceIdType.MESH
F32 = jnp.float32
BF16 = jnp.bfloat16

UNIT = 8.0 / 5.0
CENTRE = 3.0 * (-205.0 / 72.0) / UNIT
FAR = 1.0 / 63.0
EDGE = 4


def band(width):
    gap = np.abs(np.arange(width)[:, None] - np.arange(width)[None, :])
    near = np.where(gap == 1, 1.0, 0.0) + np.where(gap == 2, -1.0 / 8.0, 0.0)
    far = np.where(gap == 3, 1.0, 0.0) + np.where(gap == 4, -9.0 / 128.0, 0.0)
    row = np.concatenate([near, far], axis=1)
    return np.concatenate([row, row], axis=0)


def place():
    shot = lax.axis_index("shot")
    slab = lax.axis_index("slab")
    return shot, slab, lax.rem(shot, 2), lax.rem(slab, 2)


def gather_kernel(
    slabs, traces, cells, spots, all_traces, all_cells, all_spots, relay, send, recv, own, pair_send, pair_recv, pair_own
):
    shot, slab, core, side = place()
    half = slabs // 2
    z = lax.div(slab, 2)
    stays = core == side
    moves = core != side
    other = (shot + 1 - 2 * core, slab)
    barrier = pltpu.get_barrier_semaphore()

    def source_of(k):
        return (shot - core + lax.rem(k, 2), k)

    def is_source(k):
        return jnp.logical_and(stays, k == slab)

    @pl.loop(0, slabs)
    def _(k):
        @pl.when(jnp.logical_not(is_source(k)))
        def _():
            pl.semaphore_signal(barrier, inc=1, device_id=source_of(k), device_id_type=MESH)

    @pl.when(stays)
    def _():
        pl.semaphore_signal(barrier, inc=1, device_id=other, device_id_type=MESH)

    pl.semaphore_wait(barrier, jnp.where(stays, 2 * slabs - 1, 1))

    to_relay = pltpu.make_async_remote_copy(
        src_ref=traces,
        dst_ref=relay,
        send_sem=pair_send.at[0],
        recv_sem=pair_recv.at[0],
        device_id=other,
        device_id_type=MESH,
    )
    to_cells = pltpu.make_async_remote_copy(
        src_ref=cells,
        dst_ref=all_cells,
        send_sem=pair_send.at[1],
        recv_sem=pair_recv.at[1],
        device_id=other,
        device_id_type=MESH,
    )
    to_spots = pltpu.make_async_remote_copy(
        src_ref=spots,
        dst_ref=all_spots,
        send_sem=pair_send.at[2],
        recv_sem=pair_recv.at[2],
        device_id=other,
        device_id_type=MESH,
    )
    keep = (
        pltpu.make_async_copy(traces, all_traces.at[slab], pair_own.at[0]),
        pltpu.make_async_copy(cells, all_cells, pair_own.at[1]),
        pltpu.make_async_copy(spots, all_spots, pair_own.at[2]),
    )

    def outgoing(here, n, k, to_side):
        to_core, to_z = lax.div(k, half), lax.rem(k, half)
        return pltpu.make_async_remote_copy(
            src_ref=here,
            dst_ref=all_traces.at[slab],
            send_sem=send.at[n, k],
            recv_sem=recv.at[slab],
            device_id=(shot - core + to_core, 2 * to_z + to_side),
            device_id_type=MESH,
        )

    def is_me(k):
        return k == core * half + z

    @pl.when(moves)
    def _():
        to_relay.start()

    @pl.when(stays)
    def _():
        @pl.loop(0, slabs)
        def _(k):
            @pl.when(jnp.logical_not(is_me(k)))
            def _():
                outgoing(traces, 0, k, core).start()

        to_cells.start()
        to_spots.start()
        for copy in keep:
            copy.start()
        to_relay.wait_recv()

        @pl.loop(0, slabs)
        def _(k):
            outgoing(relay, 1, k, 1 - core).start()

    @pl.loop(0, slabs)
    def _(k):
        @pl.when(jnp.logical_not(is_source(k)))
        def _():
            pltpu.make_async_remote_copy(
                src_ref=relay,
                dst_ref=all_traces.at[k],
                send_sem=send.at[0, k],
                recv_sem=recv.at[k],
                device_id=source_of(k),
                device_id_type=MESH,
            ).wait_recv()

    @pl.when(moves)
    def _():
        to_relay.wait_send()
        to_cells.wait_recv()
        to_spots.wait_recv()

    @pl.when(stays)
    def _():
        to_cells.wait_send()
        to_spots.wait_send()
        for copy in keep:
            copy.wait()

        @pl.loop(0, slabs)
        def _(k):
            @pl.when(jnp.logical_not(is_me(k)))
            def _():
                outgoing(traces, 0, k, core).wait_send()

            outgoing(relay, 1, k, 1 - core).wait_send()


def inject_kernel(count, wide, steps, cells, traces, spots, out, amounts, mark, table, table_s, listed, sem):
    shot, slab, core, side = place()
    rows, lanes = cells.shape[1:]
    lane = lax.broadcasted_iota(jnp.int32, (rows, lanes), 1)
    order = lax.broadcasted_iota(jnp.int32, (rows, lanes), 0) * lanes + lane
    depth = cells[0] - (slab - side + core) * count
    live = jnp.logical_and(depth >= 0, depth < count)
    key = jnp.where(live, order * (1 << 18) + (depth * wide + cells[1]) * 128 + cells[2], -1)

    skipped = jnp.where(live, 0, 1)
    for bit in range(7):
        skipped = skipped + jnp.where(lane >= (1 << bit), pltpu.roll(skipped, 1 << bit, 1), 0)
    table[rows : 2 * rows] = skipped
    move = jnp.where(live, skipped, 0)
    for bit in range(7):
        from_key = pltpu.roll(key, 128 - (1 << bit), 1)
        from_move = pltpu.roll(move, 128 - (1 << bit), 1)
        comes = jnp.logical_and(
            jnp.bitwise_and(from_move, 1 << bit) != 0, jnp.logical_and(from_key >= 0, lane < 128 - (1 << bit))
        )
        goes = jnp.bitwise_and(move, 1 << bit) != 0
        key = jnp.where(comes, from_key, jnp.where(goes, -1, key))
        move = jnp.where(comes, from_move, jnp.where(goes, 0, move))
    table[0:rows] = key
    copy = pltpu.make_async_copy(table, table_s, sem.at[0])
    copy.start()

    @pl.loop(0, count * wide // 32)
    def _(i):
        out[pl.ds(pl.multiple_of(i * 256, 256), 256), :] = jnp.zeros((256, 128), F32)

    plane = wide * 128
    spot = jnp.broadcast_to(spots[:steps, 0:1], (steps, 128)).astype(jnp.int32) - (slab - side + core) * (count * plane)
    wave = jnp.broadcast_to(spots[:steps, 1:2], (steps, 128))
    tile_lane = lax.broadcasted_iota(jnp.int32, (8, 128), 1)
    tile_cell = lax.broadcasted_iota(jnp.int32, (8, 128), 0) * 128 + tile_lane
    for row in range(count):
        hit = jnp.logical_and(spot >= row * plane, spot < (row + 1) * plane)
        amounts[pl.ds(row * steps, steps), :] = jnp.where(hit, wave, 0.0)
    place_in_plane = jnp.bitwise_and(spot, plane - 1)[:8]
    for k in range(wide // 8):
        mark[pl.ds(8 * k, 8), :] = jnp.where(tile_cell + 1024 * k == place_in_plane, 1.0, 0.0)

    copy.wait()

    def gather_row(i, base):
        found = 128 - table_s[rows + i, 127]

        @pl.loop(0, lax.div(found + 15, 16))
        def _(k):
            for u in range(16):
                listed[base + 16 * k + u] = table_s[i, 16 * k + u]

        return base + found

    total = lax.fori_loop(0, rows, gather_row, jnp.int32(0))
    for u in range(8):
        listed[total + u] = -1

    @pl.loop(0, lax.div(total + 7, 8))
    def _(k):
        places, values = [], []
        for u in range(8):
            key = listed[8 * k + u]
            r = jnp.bitwise_and(lax.shift_right_logical(key, 18), rows * lanes - 1)
            cell = jnp.bitwise_and(key, (1 << 18) - 1)
            z = jnp.bitwise_and(cell, 127)
            places.append(pl.multiple_of(lax.shift_right_logical(cell, 7) * 8, 8))
            column = pl.multiple_of(jnp.bitwise_and(lax.shift_right_logical(r, 7), 1) * 128, 128)
            held = traces[lax.shift_right_logical(r, 8), :, pl.ds(column, 128)]
            turned = pltpu.roll(held, jnp.bitwise_and(z - jnp.bitwise_and(r, 127), 127), 1)
            values.append(jnp.where(tile_lane == jnp.where(key >= 0, z, -1), turned, 0.0))
        for where, value in zip(places, values):
            out[pl.ds(where, 8), :] = out[pl.ds(where, 8), :] + value


def wave_kernel(
    shots,
    slabs,
    steps,
    scale,
    adj_now,
    adj_now_far,
    adj_after,
    adj_after_far,
    state_now,
    state_before,
    speed,
    speed_far,
    added,
    amounts,
    mark,
    weights_z,
    weights_y,
    opening,
    second,
    gradient,
    qa,
    pf,
    laps,
    inj,
    spd,
    total,
    parts,
    loads,
    swap_send,
    swap_recv,
    halo_send,
    halo_recv,
    out_send,
    out_recv,
    part_send,
    part_recv,
    part_own,
):
    shot, slab, core, side = place()
    z = lax.div(slab, 2)
    stays = core == side
    moves = core != side
    count, wide, lanes = spd.shape
    mid = count - 2 * EDGE
    last = slabs // 2 - 1
    has_outer = jnp.logical_or(jnp.logical_and(core == 0, z > 0), jnp.logical_and(core == 1, z < last))
    inner = (shot + 1 - 2 * core, slab)
    outer = (shot + 1 - 2 * core, slab + 4 * core - 2)
    partner = (shot - core + side, slab - side + core)
    chunk = wide // shots
    me = shot - core + side
    own_rows = pl.ds(EDGE, count)

    def source_of(s):
        return (s - lax.rem(s, 2) + side, 2 * z + lax.rem(s, 2))

    barrier = pltpu.get_barrier_semaphore()
    pl.semaphore_signal(barrier, inc=1, device_id=inner, device_id_type=MESH)

    @pl.when(has_outer)
    def _():
        pl.semaphore_signal(barrier, inc=1, device_id=outer, device_id_type=MESH)

    @pl.when(moves)
    def _():
        pl.semaphore_signal(barrier, inc=1, device_id=partner, device_id_type=MESH)

    @pl.loop(0, shots)
    def _(s):
        @pl.when(jnp.logical_or(moves, s != shot))
        def _():
            pl.semaphore_signal(barrier, inc=1, device_id=source_of(s), device_id_type=MESH)

    def load(k, near, far, to):
        def go():
            @pl.when(stays)
            def _():
                pltpu.make_async_copy(near, to, loads.at[k]).start()

            @pl.when(moves)
            def _():
                pltpu.make_async_copy(far, to, loads.at[k]).start()

        def done():
            pltpu.make_async_copy(near, to, loads.at[k]).wait()

        return go, done

    now_go, now_done = load(0, adj_now, adj_now_far, qa.at[1, own_rows])
    after_go, after_done = load(1, adj_after, adj_after_far, qa.at[0, own_rows])
    speed_go, speed_done = load(2, speed, speed_far, spd)
    now_go()
    speed_go()
    after_go()
    inj_copy = pltpu.make_async_copy(added, inj, loads.at[3])
    inj_copy.start()

    def swap(k, here, to):
        remote = pltpu.make_async_remote_copy(
            src_ref=here,
            dst_ref=to,
            send_sem=swap_send.at[k],
            recv_sem=swap_recv.at[k],
            device_id=partner,
            device_id_type=MESH,
        )
        local = pltpu.make_async_copy(here, to, loads.at[4 + k])

        def go():
            @pl.when(moves)
            def _():
                remote.start()

            @pl.when(stays)
            def _():
                local.start()

        def done():
            @pl.when(moves)
            def _():
                remote.wait_recv()

            @pl.when(stays)
            def _():
                local.wait()

        def sent():
            @pl.when(moves)
            def _():
                remote.wait_send()

        return go, done, sent

    p_now = swap(0, state_now, pf.at[1, own_rows])
    p_before = swap(1, state_before, pf.at[0, own_rows])

    @pl.when(jnp.logical_not(has_outer))
    def _():
        @pl.loop(0, steps)
        def _(k):
            @pl.loop(0, EDGE)
            def _(r):
                row = core * (count + EDGE) + r
                qa[k + 1, row] = jnp.zeros((wide, lanes), F32)
                pf[k + 1, row] = jnp.zeros((wide, lanes), F32)

    pl.semaphore_wait(
        barrier,
        1 + jnp.where(has_outer, 1, 0) + jnp.where(moves, 1, 0) + jnp.where(stays, shots - 1, shots),
    )

    fields = (qa, pf)

    def inner_copy(chain, slot):
        return pltpu.make_async_remote_copy(
            src_ref=fields[chain].at[slot, pl.ds(count - core * mid - core * EDGE, EDGE)],
            dst_ref=fields[chain].at[slot, pl.ds(core * (count + EDGE), EDGE)],
            send_sem=halo_send.at[chain, 0, slot],
            recv_sem=halo_recv.at[chain, 0, slot],
            device_id=inner,
            device_id_type=MESH,
        )

    def outer_copy(chain, slot):
        return pltpu.make_async_remote_copy(
            src_ref=fields[chain].at[slot, pl.ds(EDGE + core * (mid + EDGE), EDGE)],
            dst_ref=fields[chain].at[slot, pl.ds((1 - core) * (count + EDGE), EDGE)],
            send_sem=halo_send.at[chain, 1, slot],
            recv_sem=halo_recv.at[chain, 1, slot],
            device_id=outer,
            device_id_type=MESH,
        )

    def send_inner(chain, slot):
        inner_copy(chain, slot).start()

    def send_outer(chain, slot):
        @pl.when(has_outer)
        def _():
            outer_copy(chain, slot).start()

    def wait_inner(chain, slot):
        inner_copy(chain, slot).wait_recv()

    def wait_outer(chain, slot):
        @pl.when(has_outer)
        def _():
            outer_copy(chain, slot).wait_recv()

    inner_base = (1 - core) * (mid + EDGE)
    outer_base = core * (mid + EDGE)

    def lateral(field, slot, group, finish):
        x = field[slot, pl.ds(EDGE + 4 * group, 4)]
        high = x.astype(BF16)
        low = (x - high.astype(F32)).astype(BF16)
        along = jnp.concatenate([high.reshape(4 * wide, lanes), low.reshape(4 * wide, lanes)], axis=1)
        across = jnp.concatenate(
            [
                jnp.concatenate([high[i] for i in range(4)], axis=1),
                jnp.concatenate([low[i] for i in range(4)], axis=1),
            ],
            axis=0,
        )
        sums_z = jnp.dot(along, weights_z[...], preferred_element_type=F32)
        sums_y = jnp.dot(weights_y[...], across, preferred_element_type=F32)
        for i in range(4):
            near = sums_z[wide * i : wide * (i + 1), :lanes] + sums_y[:wide, lanes * i : lanes * (i + 1)]
            far = sums_z[wide * i : wide * (i + 1), lanes:] + sums_y[wide:, lanes * i : lanes * (i + 1)]
            finish(4 * group + i, x[i], near + far * FAR + CENTRE * x[i])

    def depth(field, slot, base, planes, finish):
        @pl.loop(0, wide // 16)
        def _(k):
            part = pl.ds(pl.multiple_of(16 * k, 16), 16)
            e = [field[slot, base + r, part, :] for r in range(planes + 2 * EDGE)]
            for r in range(planes):
                value = (e[r + 3] + e[r + 5]) - 0.125 * (e[r + 2] + e[r + 6])
                value = value + FAR * ((e[r + 1] + e[r + 7]) - (9.0 / 128.0) * (e[r] + e[r + 8]))
                finish(base + r, part, value)

    def lateral_a(j):
        def finish(row, x, value):
            extra = inj[pl.ds(row * (8 * wide) + (steps - 1 - j), wide, stride=8), :]
            qa[j + 2, EDGE + row] = (2.0 * x - qa[j, EDGE + row]) + extra + spd[row] * value

        @pl.loop(0, count // 4)
        def _(group):
            lateral(qa, j + 1, group, finish)

        depth_a(j, EDGE, mid)

    def depth_a(j, base, planes):
        def finish(row, part, value):
            qa[j + 2, EDGE + row, part, :] = qa[j + 2, EDGE + row, part, :] + spd[row, part, :] * value

        depth(qa, j + 1, base, planes, finish)

    def edges_a(j, more):
        wait_inner(0, j + 1)
        depth_a(j, inner_base, EDGE)
        if more is None:
            send_inner(0, j + 2)
        else:
            pl.when(more)(lambda: send_inner(0, j + 2))
        wait_outer(0, j + 1)
        depth_a(j, outer_base, EDGE)
        if more is None:
            send_outer(0, j + 2)
        else:
            pl.when(more)(lambda: send_outer(0, j + 2))

    lead = steps // 2

    def lateral_f(i, kept):
        keep = i if kept else lead

        def finish(row, x, value):
            pf[i + 2, EDGE + row] = (2.0 * x - pf[i, EDGE + row]) + amounts[pl.ds(row * steps + i, 1), :] * mark[...]
            laps[keep, row] = value

        @pl.loop(0, count // 4)
        def _(group):
            lateral(pf, i + 1, group, finish)

        depth_f(i, EDGE, mid, kept)

    def depth_f(i, base, planes, kept):
        keep = i if kept else lead

        def finish(row, part, value):
            lap = laps[keep, row, part, :] + value
            pf[i + 2, EDGE + row, part, :] = pf[i + 2, EDGE + row, part, :] + spd[row, part, :] * lap
            if kept:
                laps[keep, row, part, :] = lap
            else:
                total[row, part, :] = total[row, part, :] + qa[steps - i, EDGE + row, part, :] * lap

        depth(pf, i + 1, base, planes, finish)

    def edges_f(i, kept, more):
        wait_inner(1, i + 1)
        depth_f(i, inner_base, EDGE, kept)
        if more:
            send_inner(1, i + 2)
        wait_outer(1, i + 1)
        depth_f(i, outer_base, EDGE, kept)
        if more:
            send_outer(1, i + 2)

    p_now[0]()
    now_done()
    send_outer(0, 1)
    send_inner(0, 1)
    p_before[0]()
    after_done()
    speed_done()

    @pl.loop(0, count)
    def _(row):
        spd[row] = UNIT * spd[row]

    inj_copy.wait()

    lateral_a(0)

    @pl.loop(0, lead)
    def _(j):
        edges_a(j, None)
        lateral_a(j + 1)

    p_now[1]()
    send_outer(1, 1)
    send_inner(1, 1)
    p_before[1]()
    lateral_f(0, True)

    def result(k, here, to):
        remote = pltpu.make_async_remote_copy(
            src_ref=here,
            dst_ref=to,
            send_sem=out_send.at[k],
            recv_sem=out_recv.at[k],
            device_id=partner,
            device_id_type=MESH,
        )
        local = pltpu.make_async_copy(here, to, loads.at[6 + k])

        def go():
            @pl.when(moves)
            def _():
                remote.start()

            @pl.when(stays)
            def _():
                local.start()

        def done():
            @pl.when(moves)
            def _():
                remote.wait()

            @pl.when(stays)
            def _():
                local.wait()

        return go, done

    second_out = result(0, qa.at[steps, own_rows], second.at[0])
    opening_out = result(1, qa.at[steps + 1, own_rows], opening.at[0])

    @pl.loop(0, steps - lead)
    def _(m):
        j = lead + m
        edges_a(j, j < steps - 1)

        @pl.when(j == steps - 2)
        def _():
            second_out[0]()

        edges_f(m, True, True)

        @pl.when(j < steps - 1)
        def _():
            lateral_a(j + 1)

        @pl.when(m < lead - 1)
        def _():
            lateral_f(m + 1, True)

    opening_out[0]()

    @pl.loop(0, count)
    def _(row):
        sums = qa[steps, EDGE + row] * laps[0, row]
        for i in range(1, lead):
            sums = sums + qa[steps - i, EDGE + row] * laps[i, row]
        total[row] = sums

    lateral_f(lead, False)

    @pl.loop(lead, steps - 1)
    def _(i):
        edges_f(i, False, True)
        lateral_f(i + 1, False)

    spans = ((EDGE, mid), (0, EDGE), (EDGE + mid, EDGE))

    def is_me(s):
        return jnp.logical_and(stays, s == shot)

    def part_copy(n, s):
        rows = pl.ds(*spans[n])
        return pltpu.make_async_remote_copy(
            src_ref=total.at[rows, pl.ds(pl.multiple_of(chunk * s, chunk), chunk)],
            dst_ref=parts.at[me, rows],
            send_sem=part_send.at[n, s],
            recv_sem=part_recv.at[n, me],
            device_id=(s, 2 * z + core),
            device_id_type=MESH,
        )

    def part_mine(n):
        rows = pl.ds(*spans[n])
        return pltpu.make_async_copy(
            total.at[rows, pl.ds(pl.multiple_of(chunk * shot, chunk), chunk)], parts.at[me, rows], part_own.at[n]
        )

    def send_parts(n):
        @pl.when(stays)
        def _():
            part_mine(n).start()

        @pl.loop(0, shots)
        def _(k):
            s = lax.rem(shot + k, shots)

            @pl.when(jnp.logical_not(is_me(s)))
            def _():
                part_copy(n, s).start()

    def wait_parts(n):
        rows = pl.ds(*spans[n])

        @pl.when(stays)
        def _():
            part_mine(n).wait()

        @pl.loop(0, shots)
        def _(s):
            @pl.when(jnp.logical_or(moves, s != me))
            def _():
                pltpu.make_async_remote_copy(
                    src_ref=total.at[rows, pl.ds(0, chunk)],
                    dst_ref=parts.at[s, rows],
                    send_sem=part_send.at[n, s],
                    recv_sem=part_recv.at[n, s],
                    device_id=source_of(s),
                    device_id_type=MESH,
                ).wait_recv()

            @pl.when(jnp.logical_not(is_me(s)))
            def _():
                part_copy(n, s).wait_send()

    send_parts(0)
    edges_f(steps - 1, False, False)
    send_parts(1)
    send_parts(2)

    p_now[2]()
    p_before[2]()

    @pl.loop(1, steps + 1)
    def _(slot):
        for chain in range(2):
            inner_copy(chain, slot).wait_send()

            @pl.when(has_outer)
            def _():
                outer_copy(chain, slot).wait_send()

    second_out[1]()
    opening_out[1]()
    for n in range(3):
        wait_parts(n)

    @pl.loop(0, count)
    def _(row):
        sums = parts[0, row]
        for s in range(1, shots):
            sums = sums + parts[s, row]
        gradient[row] = sums * scale


def body(
    shots,
    slabs,
    state_before,
    state_now,
    adjoint_after,
    adjoint_now,
    speed_term,
    wavelet,
    source,
    receivers,
    traces,
):
    count, wide, lanes = speed_term.shape
    steps = wavelet.shape[1]
    held = traces.shape[2]
    plane = wide * lanes
    shot, slab, core, side = place()

    over = ("shot", "slab")
    pairs, speed_pairs = [], []
    for s in range(shots):
        for k in range(slabs):
            c, d = s % 2, k % 2
            if c != d:
                pairs.append((s * slabs + k, (s - c + d) * slabs + k - d + c))
                high = (s // 2) % 2
                other = s - 2 * high + 2 * (1 - high) - c + d
                speed_pairs.append((s * slabs + k, other * slabs + k - d + c))
    now_far = lax.ppermute(adjoint_now[0], over, pairs)
    speed_far = lax.ppermute(speed_term, over, speed_pairs)
    after_far = lax.ppermute(adjoint_after[0], over, pairs)

    anywhere = pl.BlockSpec(memory_space=pl.ANY)
    in_vmem = pl.BlockSpec(memory_space=pltpu.VMEM)
    cells = receivers.reshape(3, -1, 128)
    spot = source[0, 0] * plane + source[0, 1] * lanes + source[0, 2]
    which = lax.broadcasted_iota(jnp.int32, (2 * steps, 128), 1)
    wave = jnp.concatenate([wavelet[0], wavelet[0]])[:, None]
    spots = jnp.where(which == 0, spot.astype(F32), wave)

    all_traces, all_cells, all_spots = pl.pallas_call(
        functools.partial(gather_kernel, slabs),
        name="gather_traces",
        out_shape=(
            jax.ShapeDtypeStruct((slabs, steps, held), F32),
            jax.ShapeDtypeStruct(cells.shape, jnp.int32),
            jax.ShapeDtypeStruct(spots.shape, F32),
        ),
        in_specs=[anywhere, anywhere, anywhere],
        out_specs=(in_vmem, in_vmem, in_vmem),
        scratch_shapes=[
            pltpu.VMEM((steps, held), F32),
            pltpu.SemaphoreType.DMA((2, slabs)),
            pltpu.SemaphoreType.DMA((slabs,)),
            pltpu.SemaphoreType.DMA((1,)),
            pltpu.SemaphoreType.DMA((3,)),
            pltpu.SemaphoreType.DMA((3,)),
            pltpu.SemaphoreType.DMA((3,)),
        ],
        compiler_params=pltpu.CompilerParams(collective_id=0, has_side_effects=True, vmem_limit_bytes=8 << 20),
        cost_estimate=pl.CostEstimate(flops=0, bytes_accessed=20 << 20, transcendentals=0),
    )(traces[0], cells, spots)

    added, amounts, mark = pl.pallas_call(
        functools.partial(inject_kernel, count, wide, steps),
        name="inject",
        out_shape=(
            jax.ShapeDtypeStruct((count * wide * steps, lanes), F32),
            jax.ShapeDtypeStruct((count * steps, lanes), F32),
            jax.ShapeDtypeStruct((wide, lanes), F32),
        ),
        in_specs=[in_vmem, in_vmem, in_vmem],
        out_specs=(in_vmem, in_vmem, in_vmem),
        scratch_shapes=[
            pltpu.VMEM((2 * cells.shape[1], 128), jnp.int32),
            pltpu.SMEM((2 * cells.shape[1], 128), jnp.int32),
            pltpu.SMEM((cells.size // 3 + 32,), jnp.int32),
            pltpu.SemaphoreType.DMA((1,)),
        ],
        compiler_params=pltpu.CompilerParams(vmem_limit_bytes=20 << 20),
        cost_estimate=pl.CostEstimate(flops=0, bytes_accessed=30 << 20, transcendentals=0),
    )(all_cells, all_traces, all_spots)

    weights = band(wide)

    long = count + 2 * EDGE
    opening, second, gradient = pl.pallas_call(
        functools.partial(wave_kernel, shots, slabs, steps, UNIT / (8.0 * steps)),
        name="waves",
        out_shape=(
            jax.ShapeDtypeStruct((1, count, wide, lanes), F32),
            jax.ShapeDtypeStruct((1, count, wide, lanes), F32),
            jax.ShapeDtypeStruct((count, wide // shots, lanes), F32),
        ),
        in_specs=[anywhere] * 9 + [in_vmem] * 4,
        out_specs=(in_vmem, in_vmem, in_vmem),
        scratch_shapes=[
            pltpu.VMEM((steps + 2, long, wide, lanes), F32),
            pltpu.VMEM((steps + 2, long, wide, lanes), F32),
            pltpu.VMEM((steps // 2 + 1, count, wide, lanes), F32),
            pltpu.VMEM((count * wide * steps, lanes), F32),
            pltpu.VMEM((count, wide, lanes), F32),
            pltpu.VMEM((count, wide, lanes), F32),
            pltpu.VMEM((shots, count, wide // shots, lanes), F32),
            pltpu.SemaphoreType.DMA((8,)),
            pltpu.SemaphoreType.DMA((2,)),
            pltpu.SemaphoreType.DMA((2,)),
            pltpu.SemaphoreType.DMA((2, 2, steps + 2)),
            pltpu.SemaphoreType.DMA((2, 2, steps + 2)),
            pltpu.SemaphoreType.DMA((2,)),
            pltpu.SemaphoreType.DMA((2,)),
            pltpu.SemaphoreType.DMA((3, shots)),
            pltpu.SemaphoreType.DMA((3, shots)),
            pltpu.SemaphoreType.DMA((3,)),
        ],
        compiler_params=pltpu.CompilerParams(
            collective_id=1, has_side_effects=True, vmem_limit_bytes=51 << 20
        ),
    )(
        adjoint_now[0],
        now_far,
        adjoint_after[0],
        after_far,
        state_now[0],
        state_before[0],
        speed_term,
        speed_far,
        added,
        amounts,
        mark,
        jnp.asarray(weights, BF16),
        jnp.asarray(weights.T, BF16),
    )
    return opening, second, gradient


def solution(mesh):
    return jax.shard_map(
        functools.partial(body, mesh.shape["shot"], mesh.shape["slab"]),
        mesh=mesh,
        in_specs=(
            P("shot", "slab", None, None),
            P("shot", "slab", None, None),
            P("shot", "slab", None, None),
            P("shot", "slab", None, None),
            P("slab", None, None),
            P("shot", None),
            P("shot", None),
            P("shot", None, None),
            P("shot", None, "slab"),
        ),
        out_specs=(
            P("shot", "slab", None, None),
            P("shot", "slab", None, None),
            P("slab", "shot", None),
        ),
        check_vma=False,
    )
```

```python
import functools

import jax
import jax.numpy as jnp
from jax import lax
from jax.experimental import pallas as pl
from jax.experimental.pallas import tpu as pltpu
from jax.sharding import PartitionSpec as P

MESH = pl.DeviceIdType.MESH
F32 = jnp.float32
BF16 = jnp.bfloat16

UNIT = 8.0 / 5.0
CENTRE = 3.0 * (-205.0 / 72.0) / UNIT
FAR = 1.0 / 63.0
EDGE = 4


def place():
    shot = lax.axis_index("shot")
    slab = lax.axis_index("slab")
    return shot, slab, lax.rem(shot, 2), lax.rem(slab, 2)


def gather_kernel(
    slabs,
    wide,
    lanes,
    traces,
    cells,
    source,
    wavelet,
    field,
    all_traces,
    all_cells,
    all_spots,
    field_far,
    relay,
    spots,
    send,
    recv,
    pair_send,
    pair_recv,
    pair_own,
    swap_send,
    swap_recv,
):
    shot, slab, core, side = place()
    half = slabs // 2
    z = lax.div(slab, 2)
    stays = core == side
    moves = core != side
    other = (shot + 1 - 2 * core, slab)
    barrier = pltpu.get_barrier_semaphore()

    def source_of(k):
        return (shot - core + lax.rem(k, 2), k)

    def is_source(k):
        return jnp.logical_and(stays, k == slab)

    @pl.loop(0, slabs)
    def _(k):
        @pl.when(jnp.logical_not(is_source(k)))
        def _():
            pl.semaphore_signal(barrier, inc=1, device_id=source_of(k), device_id_type=MESH)

    @pl.when(stays)
    def _():
        pl.semaphore_signal(barrier, inc=1, device_id=other, device_id_type=MESH)

    partner = (shot - core + side, slab - side + core)

    @pl.when(moves)
    def _():
        pl.semaphore_signal(barrier, inc=1, device_id=partner, device_id_type=MESH)

    steps = spots.shape[0]
    step_of = lax.broadcasted_iota(jnp.int32, spots.shape, 0)
    wave = jnp.zeros(spots.shape, F32)
    for t in range(steps):
        wave = jnp.where(step_of == t, wavelet[0, t], wave)
    cell = (source[0, 0] * (wide * lanes) + source[0, 1] * lanes + source[0, 2]).astype(F32)
    spots[...] = jnp.where(lax.broadcasted_iota(jnp.int32, spots.shape, 1) == 0, cell, wave)

    pl.semaphore_wait(barrier, jnp.where(stays, 2 * slabs - 1, 2))

    to_relay = pltpu.make_async_remote_copy(
        src_ref=traces,
        dst_ref=relay,
        send_sem=pair_send.at[0],
        recv_sem=pair_recv.at[0],
        device_id=other,
        device_id_type=MESH,
    )
    to_cells = pltpu.make_async_remote_copy(
        src_ref=cells,
        dst_ref=all_cells,
        send_sem=pair_send.at[1],
        recv_sem=pair_recv.at[1],
        device_id=other,
        device_id_type=MESH,
    )
    to_spots = pltpu.make_async_remote_copy(
        src_ref=spots,
        dst_ref=all_spots,
        send_sem=pair_send.at[2],
        recv_sem=pair_recv.at[2],
        device_id=other,
        device_id_type=MESH,
    )
    keep = (
        pltpu.make_async_copy(traces, all_traces.at[slab], pair_own.at[0]),
        pltpu.make_async_copy(cells, all_cells, pair_own.at[1]),
        pltpu.make_async_copy(spots, all_spots, pair_own.at[2]),
    )

    def outgoing(here, n, k, to_side):
        to_core, to_z = lax.div(k, half), lax.rem(k, half)
        return pltpu.make_async_remote_copy(
            src_ref=here,
            dst_ref=all_traces.at[slab],
            send_sem=send.at[n, k],
            recv_sem=recv.at[slab],
            device_id=(shot - core + to_core, 2 * to_z + to_side),
            device_id_type=MESH,
        )

    def is_me(k):
        return k == core * half + z

    swap = pltpu.make_async_remote_copy(
        src_ref=field,
        dst_ref=field_far,
        send_sem=swap_send.at[0],
        recv_sem=swap_recv.at[0],
        device_id=partner,
        device_id_type=MESH,
    )

    @pl.when(moves)
    def _():
        to_relay.start()
        swap.start()

    @pl.when(stays)
    def _():
        @pl.loop(0, slabs)
        def _(k):
            @pl.when(jnp.logical_not(is_me(k)))
            def _():
                outgoing(traces, 0, k, core).start()

        to_cells.start()
        to_spots.start()
        for copy in keep:
            copy.start()
        to_relay.wait_recv()

        @pl.loop(0, slabs)
        def _(k):
            outgoing(relay, 1, k, 1 - core).start()

    @pl.loop(0, slabs)
    def _(k):
        @pl.when(jnp.logical_not(is_source(k)))
        def _():
            pltpu.make_async_remote_copy(
                src_ref=relay,
                dst_ref=all_traces.at[k],
                send_sem=send.at[0, k],
                recv_sem=recv.at[k],
                device_id=source_of(k),
                device_id_type=MESH,
            ).wait_recv()

    @pl.when(moves)
    def _():
        swap.wait()
        to_relay.wait_send()
        to_cells.wait_recv()
        to_spots.wait_recv()

    @pl.when(stays)
    def _():
        to_cells.wait_send()
        to_spots.wait_send()
        for copy in keep:
            copy.wait()

        @pl.loop(0, slabs)
        def _(k):
            @pl.when(jnp.logical_not(is_me(k)))
            def _():
                outgoing(traces, 0, k, core).wait_send()

            outgoing(relay, 1, k, 1 - core).wait_send()


def inject_kernel(count, wide, steps, cells, traces, spots, out, table, table_s, listed, sem):
    shot, slab, core, side = place()
    rows, lanes = cells.shape[1:]
    lane = lax.broadcasted_iota(jnp.int32, (rows, lanes), 1)
    order = lax.broadcasted_iota(jnp.int32, (rows, lanes), 0) * lanes + lane
    depth = cells[0] - (slab - side + core) * count
    live = jnp.logical_and(depth >= 0, depth < count)
    key = jnp.where(live, order * (1 << 18) + (depth * wide + cells[1]) * 128 + cells[2], -1)

    skipped = jnp.where(live, 0, 1)
    for bit in range(7):
        skipped = skipped + jnp.where(lane >= (1 << bit), pltpu.roll(skipped, 1 << bit, 1), 0)
    table[rows : 2 * rows] = skipped
    move = jnp.where(live, skipped, 0)
    for bit in range(7):
        from_key = pltpu.roll(key, 128 - (1 << bit), 1)
        from_move = pltpu.roll(move, 128 - (1 << bit), 1)
        comes = jnp.logical_and(
            jnp.bitwise_and(from_move, 1 << bit) != 0, jnp.logical_and(from_key >= 0, lane < 128 - (1 << bit))
        )
        goes = jnp.bitwise_and(move, 1 << bit) != 0
        key = jnp.where(comes, from_key, jnp.where(goes, -1, key))
        move = jnp.where(comes, from_move, jnp.where(goes, 0, move))
    table[0:rows] = key
    copy = pltpu.make_async_copy(table, table_s, sem.at[0])
    copy.start()

    @pl.loop(0, count * wide // 32)
    def _(i):
        out[pl.ds(pl.multiple_of(i * 256, 256), 256), :] = jnp.zeros((256, 128), F32)

    plane = wide * 128
    spot = jnp.broadcast_to(spots[:steps, 0:1], (steps, 128)).astype(jnp.int32) - (slab - side + core) * (count * plane)
    wave = jnp.broadcast_to(spots[:steps, 1:2], (steps, 128))
    tile_lane = lax.broadcasted_iota(jnp.int32, (8, 128), 1)
    tile_cell = lax.broadcasted_iota(jnp.int32, (8, 128), 0) * 128 + tile_lane
    for row in range(count):
        hit = jnp.logical_and(spot >= row * plane, spot < (row + 1) * plane)
        out[pl.ds(count * wide * steps + row * steps, steps), :] = jnp.where(hit, wave, 0.0)
    place_in_plane = jnp.bitwise_and(spot, plane - 1)[:8]
    for k in range(wide // 8):
        out[pl.ds(count * (wide + 1) * steps + 8 * k, 8), :] = jnp.where(tile_cell + 1024 * k == place_in_plane, 1.0, 0.0)

    copy.wait()

    def gather_row(i, base):
        found = 128 - table_s[rows + i, 127]

        @pl.loop(0, lax.div(found + 15, 16))
        def _(k):
            for u in range(16):
                listed[base + 16 * k + u] = table_s[i, 16 * k + u]

        return base + found

    total = lax.fori_loop(0, rows, gather_row, jnp.int32(0))
    for u in range(8):
        listed[total + u] = -1

    @pl.loop(0, lax.div(total + 7, 8))
    def _(k):
        places, values = [], []
        for u in range(8):
            key = listed[8 * k + u]
            r = jnp.bitwise_and(lax.shift_right_logical(key, 18), rows * lanes - 1)
            cell = jnp.bitwise_and(key, (1 << 18) - 1)
            z = jnp.bitwise_and(cell, 127)
            places.append(pl.multiple_of(lax.shift_right_logical(cell, 7) * 8, 8))
            column = pl.multiple_of(jnp.bitwise_and(lax.shift_right_logical(r, 7), 1) * 128, 128)
            held = traces[lax.shift_right_logical(r, 8), :, pl.ds(column, 128)]
            turned = pltpu.roll(held, jnp.bitwise_and(z - jnp.bitwise_and(r, 127), 127), 1)
            values.append(jnp.where(tile_lane == jnp.where(key >= 0, z, -1), turned, 0.0))
        for where, value in zip(places, values):
            out[pl.ds(where, 8), :] = out[pl.ds(where, 8), :] + value


def wave_kernel(
    shots,
    slabs,
    steps,
    scale,
    adj_now,
    adj_now_far,
    adj_after,
    adj_after_far,
    state_now,
    state_before,
    speed,
    speed_far,
    added,
    opening,
    second,
    gradient,
    qa,
    pf,
    laps,
    inj,
    spd,
    total,
    parts,
    weights_z,
    weights_y,
    loads,
    swap_send,
    swap_recv,
    halo_send,
    halo_recv,
    out_send,
    out_recv,
    part_send,
    part_recv,
    part_own,
):
    shot, slab, core, side = place()
    z = lax.div(slab, 2)
    stays = core == side
    moves = core != side
    count, wide, lanes = spd.shape
    mid = count - 2 * EDGE
    last = slabs // 2 - 1
    has_outer = jnp.logical_or(jnp.logical_and(core == 0, z > 0), jnp.logical_and(core == 1, z < last))
    inner = (shot + 1 - 2 * core, slab)
    outer = (shot + 1 - 2 * core, slab + 4 * core - 2)
    partner = (shot - core + side, slab - side + core)
    chunk = wide // shots
    me = shot - core + side
    own_rows = pl.ds(EDGE, count)

    def source_of(s):
        return (s - lax.rem(s, 2) + side, 2 * z + lax.rem(s, 2))

    barrier = pltpu.get_barrier_semaphore()
    pl.semaphore_signal(barrier, inc=1, device_id=inner, device_id_type=MESH)

    @pl.when(has_outer)
    def _():
        pl.semaphore_signal(barrier, inc=1, device_id=outer, device_id_type=MESH)

    @pl.when(moves)
    def _():
        pl.semaphore_signal(barrier, inc=1, device_id=partner, device_id_type=MESH)

    @pl.loop(0, shots)
    def _(s):
        @pl.when(jnp.logical_or(moves, s != shot))
        def _():
            pl.semaphore_signal(barrier, inc=1, device_id=source_of(s), device_id_type=MESH)

    def load(k, near, far, to):
        def go():
            @pl.when(stays)
            def _():
                pltpu.make_async_copy(near, to, loads.at[k]).start()

            @pl.when(moves)
            def _():
                pltpu.make_async_copy(far, to, loads.at[k]).start()

        def done():
            pltpu.make_async_copy(near, to, loads.at[k]).wait()

        return go, done

    now_go, now_done = load(0, adj_now, adj_now_far, qa.at[1, own_rows])
    after_go, after_done = load(1, adj_after, adj_after_far, qa.at[0, own_rows])
    speed_go, speed_done = load(2, speed, speed_far, spd)
    now_go()
    speed_go()
    after_go()
    inj_copy = pltpu.make_async_copy(added, inj, loads.at[3])
    inj_copy.start()

    def swap(k, here, to):
        remote = pltpu.make_async_remote_copy(
            src_ref=here,
            dst_ref=to,
            send_sem=swap_send.at[k],
            recv_sem=swap_recv.at[k],
            device_id=partner,
            device_id_type=MESH,
        )
        local = pltpu.make_async_copy(here, to, loads.at[4 + k])

        def go():
            @pl.when(moves)
            def _():
                remote.start()

            @pl.when(stays)
            def _():
                local.start()

        def done():
            @pl.when(moves)
            def _():
                remote.wait_recv()

            @pl.when(stays)
            def _():
                local.wait()

        def sent():
            @pl.when(moves)
            def _():
                remote.wait_send()

        return go, done, sent

    p_now = swap(0, state_now, pf.at[1, own_rows])
    p_before = swap(1, state_before, pf.at[0, own_rows])

    @pl.when(jnp.logical_not(has_outer))
    def _():
        @pl.loop(0, steps)
        def _(k):
            @pl.loop(0, EDGE)
            def _(r):
                row = core * (count + EDGE) + r
                qa[k + 1, row] = jnp.zeros((wide, lanes), F32)
                pf[k + 1, row] = jnp.zeros((wide, lanes), F32)

    for across, ref in enumerate((weights_z, weights_y)):
        inside = lax.broadcasted_iota(jnp.int32, (2 * wide, 2 * wide), 0)
        given = lax.broadcasted_iota(jnp.int32, (2 * wide, 2 * wide), 1)
        if across:
            inside, given = given, inside
        gap = jnp.abs(lax.rem(inside, wide) - lax.rem(given, wide))
        near = jnp.where(gap == 1, 1.0, jnp.where(gap == 2, -1.0 / 8.0, 0.0))
        far = jnp.where(gap == 3, 1.0, jnp.where(gap == 4, -9.0 / 128.0, 0.0))
        ref[...] = jnp.where(given < wide, near, far).astype(BF16)

    pl.semaphore_wait(
        barrier,
        1 + jnp.where(has_outer, 1, 0) + jnp.where(moves, 1, 0) + jnp.where(stays, shots - 1, shots),
    )

    fields = (qa, pf)

    def inner_copy(chain, slot):
        return pltpu.make_async_remote_copy(
            src_ref=fields[chain].at[slot, pl.ds(count - core * mid - core * EDGE, EDGE)],
            dst_ref=fields[chain].at[slot, pl.ds(core * (count + EDGE), EDGE)],
            send_sem=halo_send.at[chain, 0, slot],
            recv_sem=halo_recv.at[chain, 0, slot],
            device_id=inner,
            device_id_type=MESH,
        )

    def outer_copy(chain, slot):
        return pltpu.make_async_remote_copy(
            src_ref=fields[chain].at[slot, pl.ds(EDGE + core * (mid + EDGE), EDGE)],
            dst_ref=fields[chain].at[slot, pl.ds((1 - core) * (count + EDGE), EDGE)],
            send_sem=halo_send.at[chain, 1, slot],
            recv_sem=halo_recv.at[chain, 1, slot],
            device_id=outer,
            device_id_type=MESH,
        )

    def send_inner(chain, slot):
        inner_copy(chain, slot).start()

    def send_outer(chain, slot):
        @pl.when(has_outer)
        def _():
            outer_copy(chain, slot).start()

    def wait_inner(chain, slot):
        inner_copy(chain, slot).wait_recv()

    def wait_outer(chain, slot):
        @pl.when(has_outer)
        def _():
            outer_copy(chain, slot).wait_recv()

    amounts_at = count * wide * steps
    mark_at = amounts_at + count * steps
    inner_base = (1 - core) * (mid + EDGE)
    outer_base = core * (mid + EDGE)

    def lateral(field, slot, group, finish):
        x = field[slot, pl.ds(EDGE + 4 * group, 4)]
        high = x.astype(BF16)
        low = (x - high.astype(F32)).astype(BF16)
        along = jnp.concatenate([high.reshape(4 * wide, lanes), low.reshape(4 * wide, lanes)], axis=1)
        across = jnp.concatenate(
            [
                jnp.concatenate([high[i] for i in range(4)], axis=1),
                jnp.concatenate([low[i] for i in range(4)], axis=1),
            ],
            axis=0,
        )
        sums_z = jnp.dot(along, weights_z[...], preferred_element_type=F32)
        sums_y = jnp.dot(weights_y[...], across, preferred_element_type=F32)
        for i in range(4):
            near = sums_z[wide * i : wide * (i + 1), :lanes] + sums_y[:wide, lanes * i : lanes * (i + 1)]
            far = sums_z[wide * i : wide * (i + 1), lanes:] + sums_y[wide:, lanes * i : lanes * (i + 1)]
            finish(4 * group + i, x[i], near + far * FAR + CENTRE * x[i])

    def depth(field, slot, base, planes, finish):
        @pl.loop(0, wide // 16)
        def _(k):
            part = pl.ds(pl.multiple_of(16 * k, 16), 16)
            e = [field[slot, base + r, part, :] for r in range(planes + 2 * EDGE)]
            for r in range(planes):
                value = (e[r + 3] + e[r + 5]) - 0.125 * (e[r + 2] + e[r + 6])
                value = value + FAR * ((e[r + 1] + e[r + 7]) - (9.0 / 128.0) * (e[r] + e[r + 8]))
                finish(base + r, part, value)

    def lateral_a(j):
        def finish(row, x, value):
            extra = inj[pl.ds(row * (8 * wide) + (steps - 1 - j), wide, stride=8), :]
            qa[j + 2, EDGE + row] = (2.0 * x - qa[j, EDGE + row]) + extra + spd[row] * value

        @pl.loop(0, count // 4)
        def _(group):
            lateral(qa, j + 1, group, finish)

        depth_a(j, EDGE, mid)

    def depth_a(j, base, planes):
        def finish(row, part, value):
            qa[j + 2, EDGE + row, part, :] = qa[j + 2, EDGE + row, part, :] + spd[row, part, :] * value

        depth(qa, j + 1, base, planes, finish)

    def edges_a(j, more):
        wait_inner(0, j + 1)
        depth_a(j, inner_base, EDGE)
        if more is None:
            send_inner(0, j + 2)
        else:
            pl.when(more)(lambda: send_inner(0, j + 2))
        wait_outer(0, j + 1)
        depth_a(j, outer_base, EDGE)
        if more is None:
            send_outer(0, j + 2)
        else:
            pl.when(more)(lambda: send_outer(0, j + 2))

    lead = steps // 2

    def lateral_f(i, kept):
        keep = i if kept else lead

        def finish(row, x, value):
            pf[i + 2, EDGE + row] = (2.0 * x - pf[i, EDGE + row]) + inj[pl.ds(amounts_at + row * steps + i, 1), :] * inj[pl.ds(mark_at, wide), :]
            laps[keep, row] = value

        @pl.loop(0, count // 4)
        def _(group):
            lateral(pf, i + 1, group, finish)

        depth_f(i, EDGE, mid, kept)

    def depth_f(i, base, planes, kept):
        keep = i if kept else lead

        def finish(row, part, value):
            lap = laps[keep, row, part, :] + value
            pf[i + 2, EDGE + row, part, :] = pf[i + 2, EDGE + row, part, :] + spd[row, part, :] * lap
            if kept:
                laps[keep, row, part, :] = lap
            else:
                total[row, part, :] = total[row, part, :] + qa[steps - i, EDGE + row, part, :] * lap

        depth(pf, i + 1, base, planes, finish)

    def edges_f(i, kept, more):
        wait_inner(1, i + 1)
        depth_f(i, inner_base, EDGE, kept)
        if more:
            send_inner(1, i + 2)
        wait_outer(1, i + 1)
        depth_f(i, outer_base, EDGE, kept)
        if more:
            send_outer(1, i + 2)

    p_now[0]()
    now_done()
    send_outer(0, 1)
    send_inner(0, 1)
    p_before[0]()
    after_done()
    speed_done()

    @pl.loop(0, count)
    def _(row):
        spd[row] = UNIT * spd[row]

    inj_copy.wait()

    lateral_a(0)

    @pl.loop(0, lead)
    def _(j):
        edges_a(j, None)
        lateral_a(j + 1)

    p_now[1]()
    send_outer(1, 1)
    send_inner(1, 1)
    p_before[1]()
    lateral_f(0, True)

    def result(k, here, to):
        remote = pltpu.make_async_remote_copy(
            src_ref=here,
            dst_ref=to,
            send_sem=out_send.at[k],
            recv_sem=out_recv.at[k],
            device_id=partner,
            device_id_type=MESH,
        )
        local = pltpu.make_async_copy(here, to, loads.at[6 + k])

        def go():
            @pl.when(moves)
            def _():
                remote.start()

            @pl.when(stays)
            def _():
                local.start()

        def done():
            @pl.when(moves)
            def _():
                remote.wait()

            @pl.when(stays)
            def _():
                local.wait()

        return go, done

    second_out = result(0, qa.at[steps, own_rows], second.at[0])
    opening_out = result(1, qa.at[steps + 1, own_rows], opening.at[0])

    @pl.loop(0, steps - lead)
    def _(m):
        j = lead + m
        edges_a(j, j < steps - 1)

        @pl.when(j == steps - 2)
        def _():
            second_out[0]()

        edges_f(m, True, True)

        @pl.when(j < steps - 1)
        def _():
            lateral_a(j + 1)

        @pl.when(m < lead - 1)
        def _():
            lateral_f(m + 1, True)

    opening_out[0]()

    @pl.loop(0, count)
    def _(row):
        sums = qa[steps, EDGE + row] * laps[0, row]
        for i in range(1, lead):
            sums = sums + qa[steps - i, EDGE + row] * laps[i, row]
        total[row] = sums

    lateral_f(lead, False)

    @pl.loop(lead, steps - 1)
    def _(i):
        edges_f(i, False, True)
        lateral_f(i + 1, False)

    spans = ((EDGE, mid), (0, EDGE), (EDGE + mid, EDGE))

    def is_me(s):
        return jnp.logical_and(stays, s == shot)

    def part_copy(n, s):
        rows = pl.ds(*spans[n])
        return pltpu.make_async_remote_copy(
            src_ref=total.at[rows, pl.ds(pl.multiple_of(chunk * s, chunk), chunk)],
            dst_ref=parts.at[me, rows],
            send_sem=part_send.at[n, s],
            recv_sem=part_recv.at[n, me],
            device_id=(s, 2 * z + core),
            device_id_type=MESH,
        )

    def part_mine(n):
        rows = pl.ds(*spans[n])
        return pltpu.make_async_copy(
            total.at[rows, pl.ds(pl.multiple_of(chunk * shot, chunk), chunk)], parts.at[me, rows], part_own.at[n]
        )

    def send_parts(n):
        @pl.when(stays)
        def _():
            part_mine(n).start()

        @pl.loop(0, shots)
        def _(k):
            s = lax.rem(shot + k, shots)

            @pl.when(jnp.logical_not(is_me(s)))
            def _():
                part_copy(n, s).start()

    def wait_parts(n):
        rows = pl.ds(*spans[n])

        @pl.when(stays)
        def _():
            part_mine(n).wait()

        @pl.loop(0, shots)
        def _(s):
            @pl.when(jnp.logical_or(moves, s != me))
            def _():
                pltpu.make_async_remote_copy(
                    src_ref=total.at[rows, pl.ds(0, chunk)],
                    dst_ref=parts.at[s, rows],
                    send_sem=part_send.at[n, s],
                    recv_sem=part_recv.at[n, s],
                    device_id=source_of(s),
                    device_id_type=MESH,
                ).wait_recv()

            @pl.when(jnp.logical_not(is_me(s)))
            def _():
                part_copy(n, s).wait_send()

    send_parts(0)
    edges_f(steps - 1, False, False)
    send_parts(1)
    send_parts(2)

    p_now[2]()
    p_before[2]()

    @pl.loop(1, steps + 1)
    def _(slot):
        for chain in range(2):
            inner_copy(chain, slot).wait_send()

            @pl.when(has_outer)
            def _():
                outer_copy(chain, slot).wait_send()

    second_out[1]()
    opening_out[1]()
    for n in range(3):
        wait_parts(n)

    @pl.loop(0, count)
    def _(row):
        sums = parts[0, row]
        for s in range(1, shots):
            sums = sums + parts[s, row]
        gradient[row] = sums * scale


def body(
    shots,
    slabs,
    state_before,
    state_now,
    adjoint_after,
    adjoint_now,
    speed_term,
    wavelet,
    source,
    receivers,
    traces,
):
    count, wide, lanes = speed_term.shape
    steps = wavelet.shape[1]
    held = traces.shape[2]
    plane = wide * lanes
    shot, slab, core, side = place()

    over = ("shot", "slab")
    pairs, speed_pairs = [], []
    for s in range(shots):
        for k in range(slabs):
            c, d = s % 2, k % 2
            if c != d:
                pairs.append((s * slabs + k, (s - c + d) * slabs + k - d + c))
                high = (s // 2) % 2
                other = s - 2 * high + 2 * (1 - high) - c + d
                speed_pairs.append((s * slabs + k, other * slabs + k - d + c))
    anywhere = pl.BlockSpec(memory_space=pl.ANY)
    in_vmem = pl.BlockSpec(memory_space=pltpu.VMEM)
    in_smem = pl.BlockSpec(memory_space=pltpu.SMEM)
    cells = receivers.reshape(3, -1, 128)

    all_traces, all_cells, all_spots, now_far = pl.pallas_call(
        functools.partial(gather_kernel, slabs, wide, lanes),
        name="gather_traces",
        out_shape=(
            jax.ShapeDtypeStruct((slabs, steps, held), F32),
            jax.ShapeDtypeStruct(cells.shape, jnp.int32),
            jax.ShapeDtypeStruct((steps, 128), F32),
            jax.ShapeDtypeStruct(speed_term.shape, F32),
        ),
        in_specs=[anywhere, anywhere, in_smem, in_smem, anywhere],
        out_specs=(in_vmem, in_vmem, in_vmem, anywhere),
        scratch_shapes=[
            pltpu.VMEM((steps, held), F32),
            pltpu.VMEM((steps, 128), F32),
            pltpu.SemaphoreType.DMA((2, slabs)),
            pltpu.SemaphoreType.DMA((slabs,)),
            pltpu.SemaphoreType.DMA((3,)),
            pltpu.SemaphoreType.DMA((3,)),
            pltpu.SemaphoreType.DMA((3,)),
            pltpu.SemaphoreType.DMA((1,)),
            pltpu.SemaphoreType.DMA((1,)),
        ],
        compiler_params=pltpu.CompilerParams(collective_id=0, has_side_effects=True, vmem_limit_bytes=67_000_000),
        cost_estimate=pl.CostEstimate(flops=0, bytes_accessed=20 << 20, transcendentals=0),
    )(traces[0], cells, source, wavelet, adjoint_now[0])

    after, here_speed, all_traces = lax.optimization_barrier((adjoint_after[0], speed_term, all_traces))
    after_far = lax.ppermute(after, over, pairs)
    speed_far = lax.ppermute(here_speed, over, speed_pairs)

    held_rows = count * (wide + 1) * steps + wide
    added = pl.pallas_call(
        functools.partial(inject_kernel, count, wide, steps),
        name="inject",
        out_shape=jax.ShapeDtypeStruct((held_rows, lanes), F32),
        in_specs=[in_vmem, in_vmem, in_vmem],
        out_specs=in_vmem,
        scratch_shapes=[
            pltpu.VMEM((2 * cells.shape[1], 128), jnp.int32),
            pltpu.SMEM((2 * cells.shape[1], 128), jnp.int32),
            pltpu.SMEM((cells.size // 3 + 32,), jnp.int32),
            pltpu.SemaphoreType.DMA((1,)),
        ],
        compiler_params=pltpu.CompilerParams(vmem_limit_bytes=67_000_000),
        cost_estimate=pl.CostEstimate(flops=0, bytes_accessed=30 << 20, transcendentals=0),
    )(all_cells, all_traces, all_spots)

    long = count + 2 * EDGE
    opening, second, gradient = pl.pallas_call(
        functools.partial(wave_kernel, shots, slabs, steps, UNIT / (8.0 * steps)),
        name="waves",
        out_shape=(
            jax.ShapeDtypeStruct((1, count, wide, lanes), F32),
            jax.ShapeDtypeStruct((1, count, wide, lanes), F32),
            jax.ShapeDtypeStruct((count, wide // shots, lanes), F32),
        ),
        in_specs=[anywhere] * 9,
        out_specs=(in_vmem, in_vmem, in_vmem),
        scratch_shapes=[
            pltpu.VMEM((steps + 2, long, wide, lanes), F32),
            pltpu.VMEM((steps + 2, long, wide, lanes), F32),
            pltpu.VMEM((steps // 2 + 1, count, wide, lanes), F32),
            pltpu.VMEM((held_rows, lanes), F32),
            pltpu.VMEM((count, wide, lanes), F32),
            pltpu.VMEM((count, wide, lanes), F32),
            pltpu.VMEM((shots, count, wide // shots, lanes), F32),
            pltpu.VMEM((2 * wide, 2 * wide), BF16),
            pltpu.VMEM((2 * wide, 2 * wide), BF16),
            pltpu.SemaphoreType.DMA((8,)),
            pltpu.SemaphoreType.DMA((2,)),
            pltpu.SemaphoreType.DMA((2,)),
            pltpu.SemaphoreType.DMA((2, 2, steps + 2)),
            pltpu.SemaphoreType.DMA((2, 2, steps + 2)),
            pltpu.SemaphoreType.DMA((2,)),
            pltpu.SemaphoreType.DMA((2,)),
            pltpu.SemaphoreType.DMA((3, shots)),
            pltpu.SemaphoreType.DMA((3, shots)),
            pltpu.SemaphoreType.DMA((3,)),
        ],
        compiler_params=pltpu.CompilerParams(
            collective_id=1, has_side_effects=True, vmem_limit_bytes=51 << 20
        ),
    )(
        adjoint_now[0],
        now_far,
        adjoint_after[0],
        after_far,
        state_now[0],
        state_before[0],
        speed_term,
        speed_far,
        added,
    )
    return opening, second, gradient


def solution(mesh):
    return jax.shard_map(
        functools.partial(body, mesh.shape["shot"], mesh.shape["slab"]),
        mesh=mesh,
        in_specs=(
            P("shot", "slab", None, None),
            P("shot", "slab", None, None),
            P("shot", "slab", None, None),
            P("shot", "slab", None, None),
            P("slab", None, None),
            P("shot", None),
            P("shot", None),
            P("shot", None, None),
            P("shot", None, "slab"),
        ),
        out_specs=(
            P("shot", "slab", None, None),
            P("shot", "slab", None, None),
            P("slab", "shot", None),
        ),
        check_vma=False,
    )
```
